32 devices in a mesh: groups: 2 (over y), ctx: 8 (over z, x), col: 2 (over core).
Axes of the slice: x: 2, y: 2, z: 4, core: 2. Of those that a mesh axis runs over, the one named last changes fastest.
Arguments:
- activations: bfloat16 [2048, 4096], P(('groups', 'ctx'), 'col'), parts along dimension 0, may hold values from -6 to 6
- gradients: bfloat16 [2048, 14336], P(('groups', 'ctx'), 'col'), parts along dimension 0, may hold values from -6 to 6
- doc_ids: int32 [2048], P(('groups', 'ctx')), parts along dimension 0, may hold values from 0 to 11, as said below
- proj_in: bfloat16 [4096, 64], P('col'), may hold values from -0.046875 to 0.046875
- proj_out: bfloat16 [14336, 64], P('col'), may hold values from -0.0234375 to 0.0234375
- inverse: float32 [4096, 4096], P('col', 'ctx')
- store_rows: bfloat16 [2048, 4096], P(('groups', 'ctx', 'col')), parts along dimension 0, may hold values from -0.09375 to 0.09375
Outputs:
- scores: float32 [12, 2048], P(None, ('groups', 'ctx', 'col')), parts along dimension 1
The draws below stay inside these ranges and needn't reach their ends.
There are 2 independent parts, one for each index of `groups`. The reference program is written for one: setup_inputs(seed, part) draws one part's arguments, and reference() takes and returns one part's arrays. A program takes and returns all parts, laid end to end along the dimension named above; an argument that names none is the same for every part. Nothing has to cross between parts.
Inputs may be any that keep to these rules, and one draw needn't show every extreme that they name: `doc_ids`: document numbers never fall and rise by at most one from a token to the next, starting at 0. Every aligned block of 128 tokens holds the last token of one or two documents; the last token of the sequence ends document 12 - 1.
All inputs are finite; a program needn't handle non-finite values.
Results may differ from the reference program's by a relative error of at most 0.0029.
Values may be sent and summed in bfloat16 or wider, within the bound.
A program may use at most 64 MiB of HBM per device.

```python
import jax
import jax.numpy as jnp
from jax import lax

D = 4096
FF = 14336
R = 64
F = 4096
TOK_DEV = 128
TOKENS = 1024
NDOC = 12
STORE = 1024


def draw_doc_ids(key, part):
    block_count = TOKENS // TOK_DEV
    key_perm = jax.random.fold_in(key, 11)
    key_late = jax.random.fold_in(key, 12)
    key_early = jax.random.fold_in(key, 13)
    ranking = jax.random.permutation(key_perm, block_count)
    has_two = ranking < block_count // 2
    late_end = jax.random.randint(key_late, (block_count,), TOK_DEV // 2, TOK_DEV)
    late_end = jnp.where(jnp.arange(block_count) == block_count - 1, TOK_DEV - 1, late_end)
    early_end = jax.random.randint(key_early, (block_count,), 0, TOK_DEV // 2)
    position = jnp.arange(TOK_DEV)[None, :]
    is_end = (position == late_end[:, None]) | has_two[:, None] & (position == early_end[:, None])
    flat_end = is_end.reshape(TOKENS).astype(jnp.int32)
    return (jnp.cumsum(flat_end) - flat_end).astype(jnp.int32)


def draw_inverse(key, part):
    key_diag = jax.random.fold_in(key, 21)
    key_off = jax.random.fold_in(key, 22)
    diagonal = jnp.exp(jax.random.uniform(key_diag, (F,), jnp.float32, jnp.log(0.5), jnp.log(2.0)))
    offdiag = jax.random.normal(key_off, (F, F), jnp.float32) * (0.5 / jnp.sqrt(jnp.float32(F)))
    matrix = offdiag + jnp.diag(diagonal)
    return matrix.astype(jnp.float32)


def steps_of(rng, dims, cuts, low, largest):
    factor_of = 1.0
    for axis_at, blocks in cuts:
        steps = jax.random.uniform(jax.random.fold_in(jax.random.fold_in(rng, 6), axis_at), (blocks,), jnp.float32, low / len(cuts), largest / len(cuts))
        factor_of = factor_of * jnp.repeat(jnp.exp(steps), dims[axis_at] // blocks).reshape((-1,) + (1,) * (len(dims) - 1 - axis_at))
    return factor_of


def centred(key, shape, deviation, most, cuts=(), kind=jnp.bfloat16):
    level = steps_of(key, shape, cuts, -0.22, 0.18) if cuts else 1.0
    result = jax.random.normal(key, shape, jnp.float32) * deviation * level
    return jnp.minimum(jnp.maximum(result, -most), most).astype(kind)


def setup_inputs(seed: int = 0, part: int = 0) -> dict:
    keys = jax.random.split(jax.random.key(seed), 8)
    part_keys = jax.random.split(jax.random.fold_in(keys[7], part), 8)
    activations = centred(part_keys[0], (TOKENS, D), 1.0, 6.0, ((0, 8), (1, 2)))
    gradients = centred(part_keys[1], (TOKENS, FF), 1.0, 6.0, ((0, 8), (1, 2)))
    doc_ids = draw_doc_ids(jax.random.fold_in(jax.random.fold_in(keys[7], part), 71), part)
    proj_in = centred(keys[3], (D, R), (4 * D) ** -0.5, 0.046875, ((0, 2),))
    proj_out = centred(keys[4], (FF, R), (4 * FF) ** -0.5, 0.0234375, ((0, 2),))
    inverse = draw_inverse(jax.random.fold_in(keys[7], 71), part)
    store_rows = centred(part_keys[6], (STORE, F), F ** -0.5, 0.09375, ((0, 16),))
    return {"activations": activations, "gradients": gradients, "doc_ids": doc_ids, "proj_in": proj_in, "proj_out": proj_out, "inverse": inverse, "store_rows": store_rows}


def reference(activations, gradients, doc_ids, proj_in, proj_out, inverse, store_rows):
    proj_left = jnp.dot(activations, proj_in, preferred_element_type=jnp.float32)
    proj_right = jnp.dot(gradients, proj_out, preferred_element_type=jnp.float32)
    token_count = proj_left.shape[0]
    proj_rank = proj_left.shape[1]
    col_blocks = proj_left.reshape(token_count, proj_rank // 8, 8).transpose(1, 0, 2)

    def per_block(block_left):
        outer_rows = (block_left[:, :, None] * proj_right[:, None, :]).reshape(token_count, 8 * proj_rank)
        return jax.ops.segment_sum(outer_rows, doc_ids, num_segments=NDOC)

    block_sums = lax.map(per_block, col_blocks)
    doc_grads = block_sums.transpose(1, 0, 2).reshape(NDOC, proj_rank * proj_rank)
    precond = jnp.dot(doc_grads, inverse, precision=lax.Precision.HIGHEST, preferred_element_type=jnp.float32).astype(jnp.bfloat16)
    return jnp.dot(precond, store_rows.T, preferred_element_type=jnp.float32)
```

```python
import functools

import jax
import jax.numpy as jnp
from jax import lax
from jax.experimental import pallas as pl
from jax.experimental.pallas import tpu as pltpu
from jax.sharding import PartitionSpec as P


def from_behind(block, axis, distance):
    devices = range(lax.axis_size(axis))
    route = [(i - distance, i) for i in devices if i - distance in devices]
    return lax.ppermute(block, axis, route)


def shards(activations, gradients, doc_ids, proj_in, proj_out, inverse, store_rows):
    left_part = jnp.dot(activations, proj_in, preferred_element_type=jnp.float32)
    right_part = jnp.dot(gradients, proj_out, preferred_element_type=jnp.float32)
    proj_left, proj_right = lax.psum((left_part, right_part), "col")
    proj_rank = proj_right.shape[1]
    half_rank = proj_rank // lax.axis_size("col")
    own_half = lax.dynamic_slice_in_dim(proj_left, lax.axis_index("col") * half_rank, half_rank, 1)
    first_doc = doc_ids[0]
    slot_index = doc_ids - first_doc
    onehot = (slot_index[:, None] == jnp.arange(3, dtype=jnp.int32)[None, :]).astype(jnp.float32)
    weighted = (onehot[:, :, None] * own_half[:, None, :]).reshape(own_half.shape[0], 3 * half_rank)
    local_sums = lax.dot_general(
        weighted,
        proj_right,
        (((0,), (0,)), ((), ())),
        precision=lax.Precision.HIGHEST,
        preferred_element_type=jnp.float32,
    ).reshape(3, half_rank * proj_rank)
    doc_count = 3 * lax.axis_size("ctx") // 2
    last_row = lax.dynamic_index_in_dim(local_sums, slot_index[-1], 0, keepdims=False)
    incoming, incoming_id = from_behind((last_row, doc_ids[-1].astype(jnp.float32)), "ctx", 1)
    matches = (incoming_id == first_doc.astype(jnp.float32)).astype(jnp.float32)
    head_row = local_sums[0] + matches * incoming
    owned_rows = jnp.stack([head_row, local_sums[1]])
    owned_ids = (first_doc + jnp.arange(2, dtype=jnp.int32)).astype(jnp.float32)
    gathered, gathered_ids = (
        lax.all_gather(owned_rows, "ctx", axis=0, tiled=True),
        lax.all_gather(owned_ids, "ctx", axis=0, tiled=True),
    )
    positions = jnp.arange(gathered.shape[0], dtype=jnp.int32)
    wanted = jnp.arange(doc_count, dtype=jnp.int32).astype(jnp.float32)
    found = gathered_ids[None, :] == wanted[:, None]
    chosen = jnp.max(jnp.where(found, positions[None, :], -1), axis=1)
    doc_grads = jnp.take(gathered, chosen, axis=0)
    partial_q = jnp.dot(
        doc_grads, inverse, precision=lax.Precision.HIGHEST, preferred_element_type=jnp.float32
    )
    precond = lax.psum(partial_q, "col").astype(jnp.bfloat16)
    return lax.dot_general(
        lax.all_gather(precond, "ctx", axis=1, tiled=True),
        store_rows,
        (((1,), (1,)), ((), ())),
        preferred_element_type=jnp.float32,
    )


LANES = 128
SLOTS = 3
CHUNKS = 4
MESH = pl.DeviceIdType.MESH
NT = (((1,), (1,)), ((), ()))


def halves(value):
    high = value.astype(jnp.bfloat16).astype(jnp.float32)
    return high, value - high


def dot_nt(left, right):
    return lax.dot_general(left, right, NT, preferred_element_type=jnp.float32)


def score_kernel(
    n, cols, docs,
    act, grad, ids, pin, pout, inv, store, out,
    act_v, grad_v, pin_v, pout_v, inv_v, store_v, inv_hi, inv_lo,
    ids_all, part_l, part_r, from_l, from_r, full_l, sums, q_part, q_from, q_all,
    load_sem, ids_send, ids_recv, pair_send, pair_recv, sums_send, sums_recv, q_send, q_recv,
):
    me = lax.axis_index("ctx")
    core = lax.axis_index("col")
    other = cols - 1 - core
    rank = pin.shape[0]
    half = rank // cols
    pack = LANES // rank
    groups = half // pack
    piece = SLOTS * groups
    width = q_part.shape[2]

    loads = [
        pltpu.make_async_copy(ids, ids_all.at[me], load_sem.at[0]),
        pltpu.make_async_copy(act, act_v, load_sem.at[1]),
        pltpu.make_async_copy(pin, pin_v, load_sem.at[2]),
    ]
    step = grad.shape[1] // CHUNKS
    for i in range(CHUNKS):
        span = pl.ds(i * step, step)
        loads.append(pltpu.make_async_copy(pout.at[:, span], pout_v.at[:, span], load_sem.at[3 + 2 * i]))
        loads.append(pltpu.make_async_copy(grad.at[:, span], grad_v.at[:, span], load_sem.at[4 + 2 * i]))
    loads.append(pltpu.make_async_copy(inv, inv_v, load_sem.at[3 + 2 * CHUNKS]))
    loads.append(pltpu.make_async_copy(store, store_v, load_sem.at[4 + 2 * CHUNKS]))
    for load in loads:
        load.start()

    barrier = pltpu.get_barrier_semaphore()
    peers = []
    for r in range(n):
        for d in range(cols):
            if r or d:
                peers.append({"ctx": lax.rem(me + r, n), "col": lax.rem(core + d, cols)})
    for peer in peers:
        pl.semaphore_signal(barrier, inc=1, device_id=peer, device_id_type=MESH)

    loads[1].wait()
    loads[2].wait()
    part_l[...] = dot_nt(pin_v[...], act_v[...])
    pl.semaphore_wait(barrier, len(peers))

    def remote(src, dst, send, recv, peer):
        copy = pltpu.make_async_remote_copy(
            src_ref=src, dst_ref=dst, send_sem=send, recv_sem=recv, device_id=peer, device_id_type=MESH
        )
        copy.start()
        return copy

    partner = {"col": other}
    copy_l = remote(part_l.at[pl.ds(other * half, half)], from_l, pair_send.at[0], pair_recv.at[0], partner)
    ids_copies = [
        remote(ids, ids_all.at[me], ids_send.at[r], ids_recv.at[r], {"ctx": lax.rem(me + r, n)})
        for r in range(1, n)
    ]

    right = None
    for i in range(CHUNKS):
        span = pl.ds(i * step, step)
        loads[3 + 2 * i].wait()
        loads[4 + 2 * i].wait()
        term = dot_nt(pout_v[:, span], grad_v[:, span])
        right = term if right is None else right + term
    part_r[...] = right
    copy_r = remote(part_r, from_r, pair_send.at[1], pair_recv.at[1], partner)

    loads[0].wait()
    own_ids = ids_all[me]
    first = own_ids[:, 0:1]
    masks = [(own_ids == first + s).astype(jnp.float32) for s in range(SLOTS)]
    copy_l.wait_recv()
    full_l[...] = part_l[pl.ds(pl.multiple_of(core * half, half), half), :] + from_l[...]
    highs, lows = [], []
    for p in range(pack):
        rows = full_l[pl.ds(p, groups, stride=pack), :]
        high, low = halves(jnp.concatenate([rows * mask for mask in masks], axis=0))
        highs.append(high)
        lows.append(low)
    weights = jnp.concatenate(highs + highs + lows, axis=1).astype(jnp.bfloat16)
    copy_r.wait_recv()
    high, low = halves(part_r[...] + from_r[...])
    zero = jnp.zeros_like(high)

    def diagonal(block, p):
        return [block if q == p else zero for q in range(pack)]

    spread = jnp.concatenate(
        [
            jnp.concatenate(diagonal(high, p) + diagonal(low, p) + diagonal(high, p), axis=1)
            for p in range(pack)
        ],
        axis=0,
    ).astype(jnp.bfloat16)
    mine = pl.ds(pl.multiple_of(me * piece, 8), piece)
    sums[mine, :] = dot_nt(weights, spread)
    sums_copies = [
        remote(sums.at[mine], sums.at[mine], sums_send.at[r], sums_recv.at[r], {"ctx": lax.rem(me + r, n)})
        for r in sorted(range(1, n), key=lambda r: -min(r, n - r))
    ]

    loads[3 + 2 * CHUNKS].wait()
    band = LANES

    def split(i, carry):
        rows = pl.ds(pl.multiple_of(i * band, band), band)
        high, low = halves(inv_v[rows, :])
        inv_hi[rows, :] = high.astype(jnp.bfloat16)
        inv_lo[rows, :] = low.astype(jnp.bfloat16)
        return carry

    lax.fori_loop(0, inv_v.shape[0] // band, split, 0)

    for copy in ids_copies:
        copy.wait_recv()
    doc_rows = q_part.shape[1]
    column = lax.broadcasted_iota(jnp.int32, (1, SLOTS * n), 1)
    doc_of = jnp.zeros((1, SLOTS * n), jnp.int32)
    for b in range(n):
        inside = (column >= b * SLOTS) & (column < (b + 1) * SLOTS)
        doc_of = jnp.where(inside, ids_all[b][:, 0:1] + (column - b * SLOTS), doc_of)
    pick = (lax.broadcasted_iota(jnp.int32, (doc_rows, SLOTS * n), 0) == doc_of).astype(jnp.float32)

    for copy in sums_copies:
        copy.wait_recv()
    gathered = jnp.concatenate(
        [sums[pl.ds(k, SLOTS * n, stride=groups), :] for k in range(groups)], axis=1
    )
    high, low = halves(gathered)
    both = jnp.concatenate([high, low], axis=0).astype(jnp.bfloat16)
    main = jnp.dot(both, inv_hi[...], preferred_element_type=jnp.float32)
    rest = jnp.dot(high.astype(jnp.bfloat16), inv_lo[...], preferred_element_type=jnp.float32)
    rows = main[: SLOTS * n] + main[SLOTS * n :] + rest
    picked = jnp.dot(pick, rows, precision=lax.Precision.HIGHEST, preferred_element_type=jnp.float32)
    for c in range(cols):
        q_part[c] = picked[:, c * width : (c + 1) * width]
    copy_q = remote(q_part.at[other], q_from, pair_send.at[2], pair_recv.at[2], partner)
    copy_q.wait_recv()
    slot = me * cols + core
    q_all[slot] = (q_part[core] + q_from[...]).astype(jnp.bfloat16)
    q_copies = [
        remote(q_all.at[slot], q_all.at[slot], q_send.at[i], q_recv.at[i], peers[i])
        for i in sorted(range(len(peers)), key=lambda i: -min((i + 1) // cols, n - (i + 1) // cols))
    ]
    loads[4 + 2 * CHUNKS].wait()
    for copy in q_copies:
        copy.wait_recv()
    precond = jnp.concatenate([q_all[i] for i in range(n * cols)], axis=1)
    out[...] = dot_nt(precond, store_v[...])[:docs]
    for copy in [copy_l, copy_r, copy_q] + ids_copies + sums_copies + q_copies:
        copy.wait_send()


def fused(n, cols, activations, gradients, doc_ids, proj_in, proj_out, inverse, store_rows):
    tokens = activations.shape[0]
    rank = proj_in.shape[1]
    half = rank // cols
    docs = SLOTS * n // 2
    doc_rows = -(-docs // 16) * 16
    width = inverse.shape[1] // cols
    piece = SLOTS * half * rank // LANES
    anywhere = pl.BlockSpec(memory_space=pl.ANY)
    dma = pltpu.SemaphoreType.DMA
    return pl.pallas_call(
        functools.partial(score_kernel, n, cols, docs),
        name="scores",
        out_shape=jax.ShapeDtypeStruct((docs, store_rows.shape[0]), jnp.float32),
        in_specs=[anywhere] * 7,
        out_specs=pl.BlockSpec(memory_space=pltpu.VMEM),
        scratch_shapes=[
            pltpu.VMEM(activations.shape, jnp.bfloat16),
            pltpu.VMEM(gradients.shape, jnp.bfloat16),
            pltpu.VMEM(proj_in.shape[::-1], jnp.bfloat16),
            pltpu.VMEM(proj_out.shape[::-1], jnp.bfloat16),
            pltpu.VMEM(inverse.shape, jnp.float32),
            pltpu.VMEM(store_rows.shape, jnp.bfloat16),
            pltpu.VMEM(inverse.shape, jnp.bfloat16),
            pltpu.VMEM(inverse.shape, jnp.bfloat16),
            pltpu.VMEM((n, 1, tokens), jnp.int32),
            pltpu.VMEM((rank, tokens), jnp.float32),
            pltpu.VMEM((rank, tokens), jnp.float32),
            pltpu.VMEM((half, tokens), jnp.float32),
            pltpu.VMEM((rank, tokens), jnp.float32),
            pltpu.VMEM((half, tokens), jnp.float32),
            pltpu.VMEM((n * piece, LANES), jnp.float32),
            pltpu.VMEM((cols, doc_rows, width), jnp.float32),
            pltpu.VMEM((doc_rows, width), jnp.float32),
            pltpu.VMEM((n * cols, doc_rows, width), jnp.bfloat16),
            dma((5 + 2 * CHUNKS,)),
            dma((n,)), dma((n,)),
            dma((3,)), dma((3,)),
            dma((n,)), dma((n,)),
            dma((n * cols,)), dma((n * cols,)),
        ],
        compiler_params=pltpu.CompilerParams(
            collective_id=0, has_side_effects=True, vmem_limit_bytes=60 << 20
        ),
    )(activations, gradients, doc_ids[None, :], proj_in.T, proj_out.T, inverse, store_rows)


def suits_kernel(n, cols, activations, gradients, proj_in, inverse):
    rank = proj_in.shape[1]
    return (
        cols == 2
        and activations.shape[0] == LANES
        and LANES % rank == 0
        and (rank // cols * rank) % (8 * LANES) == 0
        and gradients.shape[1] % (CHUNKS * LANES) == 0
        and inverse.shape[1] % (cols * LANES) == 0
        and n <= 16
    )


def solution(mesh):
    in_specs = (
        P(("groups", "ctx"), "col"),
        P(("groups", "ctx"), "col"),
        P(("groups", "ctx")),
        P("col", None),
        P("col", None),
        P("col", "ctx"),
        P(("groups", "ctx", "col"), None),
    )
    out_specs = P(None, ("groups", "ctx", "col"))
    n, cols = mesh.shape["ctx"], mesh.shape["col"]

    def body(activations, gradients, doc_ids, proj_in, proj_out, inverse, store_rows):
        args = (activations, gradients, doc_ids, proj_in, proj_out, inverse, store_rows)
        if suits_kernel(n, cols, activations, gradients, proj_in, inverse):
            return fused(n, cols, *args)
        return shards(*args)

    return jax.shard_map(body, mesh=mesh, in_specs=in_specs, out_specs=out_specs, check_vma=False)
```

```python
import functools

import jax
import jax.numpy as jnp
from jax import lax
from jax.experimental import pallas as pl
from jax.experimental.pallas import tpu as pltpu
from jax.sharding import PartitionSpec as P


def from_behind(block, axis, distance):
    devices = range(lax.axis_size(axis))
    route = [(i - distance, i) for i in devices if i - distance in devices]
    return lax.ppermute(block, axis, route)


def shards(activations, gradients, doc_ids, proj_in, proj_out, inverse, store_rows):
    left_part = jnp.dot(activations, proj_in, preferred_element_type=jnp.float32)
    right_part = jnp.dot(gradients, proj_out, preferred_element_type=jnp.float32)
    proj_left, proj_right = lax.psum((left_part, right_part), "col")
    proj_rank = proj_right.shape[1]
    half_rank = proj_rank // lax.axis_size("col")
    own_half = lax.dynamic_slice_in_dim(proj_left, lax.axis_index("col") * half_rank, half_rank, 1)
    first_doc = doc_ids[0]
    slot_index = doc_ids - first_doc
    onehot = (slot_index[:, None] == jnp.arange(3, dtype=jnp.int32)[None, :]).astype(jnp.float32)
    weighted = (onehot[:, :, None] * own_half[:, None, :]).reshape(own_half.shape[0], 3 * half_rank)
    local_sums = lax.dot_general(
        weighted,
        proj_right,
        (((0,), (0,)), ((), ())),
        precision=lax.Precision.HIGHEST,
        preferred_element_type=jnp.float32,
    ).reshape(3, half_rank * proj_rank)
    doc_count = 3 * lax.axis_size("ctx") // 2
    last_row = lax.dynamic_index_in_dim(local_sums, slot_index[-1], 0, keepdims=False)
    incoming, incoming_id = from_behind((last_row, doc_ids[-1].astype(jnp.float32)), "ctx", 1)
    matches = (incoming_id == first_doc.astype(jnp.float32)).astype(jnp.float32)
    head_row = local_sums[0] + matches * incoming
    owned_rows = jnp.stack([head_row, local_sums[1]])
    owned_ids = (first_doc + jnp.arange(2, dtype=jnp.int32)).astype(jnp.float32)
    gathered, gathered_ids = (
        lax.all_gather(owned_rows, "ctx", axis=0, tiled=True),
        lax.all_gather(owned_ids, "ctx", axis=0, tiled=True),
    )
    positions = jnp.arange(gathered.shape[0], dtype=jnp.int32)
    wanted = jnp.arange(doc_count, dtype=jnp.int32).astype(jnp.float32)
    found = gathered_ids[None, :] == wanted[:, None]
    chosen = jnp.max(jnp.where(found, positions[None, :], -1), axis=1)
    doc_grads = jnp.take(gathered, chosen, axis=0)
    partial_q = jnp.dot(
        doc_grads, inverse, precision=lax.Precision.HIGHEST, preferred_element_type=jnp.float32
    )
    precond = lax.psum(partial_q, "col").astype(jnp.bfloat16)
    return lax.dot_general(
        lax.all_gather(precond, "ctx", axis=1, tiled=True),
        store_rows,
        (((1,), (1,)), ((), ())),
        preferred_element_type=jnp.float32,
    )


LANES = 128
SLOTS = 3
CHUNKS = 4
MESH = pl.DeviceIdType.MESH
def sums_order(n):
    order = []
    for r in range(1, n // 2 + 1):
        order += [n - r, r] if n - r != r else [r]
    return order


def q_order(n):
    return sums_order(n) + [0]


NT = (((1,), (1,)), ((), ()))


def halves(value):
    high = value.astype(jnp.bfloat16).astype(jnp.float32)
    return high, value - high


def dot_nt(left, right):
    return lax.dot_general(left, right, NT, preferred_element_type=jnp.float32)


def score_kernel(
    n, cols, docs,
    act, grad, ids, pin, pout, inv, store, out,
    act_v, grad_v, pin_v, pout_v, inv_v, store_v, inv_hi, inv_lo,
    store_t, ids_all, part_l, part_r, from_l, from_r, full_l, sums, q_part, q_from, q_all,
    load_sem, ids_send, ids_recv, pair_send, pair_recv, sums_send, sums_recv, q_send, q_recv,
):
    me = lax.axis_index("ctx")
    core = lax.axis_index("col")
    other = cols - 1 - core
    rank = pin.shape[0]
    half = rank // cols
    pack = LANES // rank
    groups = half // pack
    piece = SLOTS * groups
    width = q_part.shape[2]

    loads = [
        pltpu.make_async_copy(ids, ids_all.at[me], load_sem.at[0]),
        pltpu.make_async_copy(act, act_v, load_sem.at[1]),
        pltpu.make_async_copy(pin, pin_v, load_sem.at[2]),
    ]
    step = grad.shape[1] // CHUNKS
    for i in range(CHUNKS):
        span = pl.ds(i * step, step)
        loads.append(pltpu.make_async_copy(pout.at[:, span], pout_v.at[:, span], load_sem.at[3 + 2 * i]))
        loads.append(pltpu.make_async_copy(grad.at[:, span], grad_v.at[:, span], load_sem.at[4 + 2 * i]))
    loads.append(pltpu.make_async_copy(inv, inv_v, load_sem.at[3 + 2 * CHUNKS]))
    loads.append(pltpu.make_async_copy(store, store_v, load_sem.at[4 + 2 * CHUNKS]))
    for load in loads:
        load.start()

    barrier = pltpu.get_barrier_semaphore()
    ctx_peers = {r: {"ctx": jnp.bitwise_xor(me, r)} for r in sums_order(n)}
    peers = {}
    for r in q_order(n):
        for d in range(cols):
            if r or d:
                peers[cols * r + d] = {"ctx": jnp.bitwise_xor(me, r), "col": jnp.bitwise_xor(core, d)}
    for peer in peers.values():
        pl.semaphore_signal(barrier, inc=1, device_id=peer, device_id_type=MESH)

    loads[1].wait()
    loads[2].wait()
    part_l[...] = dot_nt(pin_v[...], act_v[...])

    def remote(src, dst, send, recv, peer):
        copy = pltpu.make_async_remote_copy(
            src_ref=src, dst_ref=dst, send_sem=send, recv_sem=recv, device_id=peer, device_id_type=MESH
        )
        copy.start()
        return copy

    right = None
    for i in range(CHUNKS):
        span = pl.ds(i * step, step)
        loads[3 + 2 * i].wait()
        loads[4 + 2 * i].wait()
        term = dot_nt(pout_v[:, span], grad_v[:, span])
        right = term if right is None else right + term
    part_r[...] = right
    pl.semaphore_wait(barrier, len(peers))
    partner = {"col": other}
    copy_l = remote(part_l.at[pl.ds(other * half, half)], from_l, pair_send.at[0], pair_recv.at[0], partner)
    copy_r = remote(part_r, from_r, pair_send.at[1], pair_recv.at[1], partner)
    ids_copies = [
        remote(ids, ids_all.at[me], ids_send.at[r], ids_recv.at[r], ctx_peers[r])
        for r in ctx_peers
    ]

    loads[0].wait()
    own_ids = ids_all[me]
    first = own_ids[:, 0:1]
    masks = [(own_ids == first + s).astype(jnp.float32) for s in range(SLOTS)]
    copy_l.wait_recv()
    full_l[...] = part_l[pl.ds(pl.multiple_of(core * half, half), half), :] + from_l[...]
    highs, lows = [], []
    for p in range(pack):
        rows = full_l[pl.ds(p, groups, stride=pack), :]
        high, low = halves(jnp.concatenate([rows * mask for mask in masks], axis=0))
        highs.append(high)
        lows.append(low)
    weights = jnp.concatenate(highs + highs + lows, axis=1).astype(jnp.bfloat16)
    copy_r.wait_recv()
    high, low = halves(part_r[...] + from_r[...])
    zero = jnp.zeros_like(high)

    def diagonal(block, p):
        return [block if q == p else zero for q in range(pack)]

    spread = jnp.concatenate(
        [
            jnp.concatenate(diagonal(high, p) + diagonal(low, p) + diagonal(high, p), axis=1)
            for p in range(pack)
        ],
        axis=0,
    ).astype(jnp.bfloat16)
    mine = pl.ds(pl.multiple_of(me * piece, 8), piece)
    sums[mine, :] = dot_nt(weights, spread)
    sums_copies = [
        remote(sums.at[mine], sums.at[mine], sums_send.at[r], sums_recv.at[r], ctx_peers[r])
        for r in ctx_peers
    ]

    loads[3 + 2 * CHUNKS].wait()
    band = LANES

    def split(i, carry):
        rows = pl.ds(pl.multiple_of(i * band, band), band)
        high, low = halves(inv_v[rows, :])
        inv_hi[rows, :] = high.astype(jnp.bfloat16)
        inv_lo[rows, :] = low.astype(jnp.bfloat16)
        return carry

    lax.fori_loop(0, inv_v.shape[0] // band, split, 0)
    loads[4 + 2 * CHUNKS].wait()
    store_t[...] = store_v[...].T

    for copy in ids_copies:
        copy.wait_recv()
    doc_rows = q_part.shape[1]
    column = lax.broadcasted_iota(jnp.int32, (1, SLOTS * n), 1)
    doc_of = jnp.zeros((1, SLOTS * n), jnp.int32)
    for b in range(n):
        inside = (column >= b * SLOTS) & (column < (b + 1) * SLOTS)
        doc_of = jnp.where(inside, ids_all[b][:, 0:1] + (column - b * SLOTS), doc_of)
    pick = (lax.broadcasted_iota(jnp.int32, (doc_rows, SLOTS * n), 0) == doc_of).astype(jnp.float32)

    for copy in sums_copies:
        copy.wait_recv()
    gathered = jnp.concatenate(
        [sums[pl.ds(k, SLOTS * n, stride=groups), :] for k in range(groups)], axis=1
    )
    high, low = halves(gathered)
    both = jnp.concatenate([high, low], axis=0).astype(jnp.bfloat16)
    main = jnp.dot(both, inv_hi[...], preferred_element_type=jnp.float32)
    rest = jnp.dot(high.astype(jnp.bfloat16), inv_lo[...], preferred_element_type=jnp.float32)
    rows = main[: SLOTS * n] + main[SLOTS * n :] + rest
    picked = jnp.dot(pick, rows, precision=lax.Precision.HIGHEST, preferred_element_type=jnp.float32)
    for c in range(cols):
        q_part[c] = picked[:, c * width : (c + 1) * width]
    copy_q = remote(q_part.at[other], q_from, pair_send.at[2], pair_recv.at[2], partner)
    copy_q.wait_recv()
    slot = me * cols + core
    q_all[slot] = (q_part[core] + q_from[...]).astype(jnp.bfloat16)
    q_copies = [
        remote(q_all.at[slot], q_all.at[slot], q_send.at[i], q_recv.at[i], peers[i])
        for i in peers
    ]
    for copy in q_copies:
        copy.wait_recv()
    precond = jnp.concatenate([q_all[i] for i in range(n * cols)], axis=1)
    out[...] = jnp.dot(precond, store_t[...], preferred_element_type=jnp.float32)[:docs]
    for copy in [copy_l, copy_r, copy_q] + ids_copies + sums_copies + q_copies:
        copy.wait_send()


def fused(n, cols, activations, gradients, doc_ids, proj_in, proj_out, inverse, store_rows):
    tokens = activations.shape[0]
    rank = proj_in.shape[1]
    half = rank // cols
    docs = SLOTS * n // 2
    doc_rows = -(-docs // 16) * 16
    width = inverse.shape[1] // cols
    piece = SLOTS * half * rank // LANES
    anywhere = pl.BlockSpec(memory_space=pl.ANY)
    dma = pltpu.SemaphoreType.DMA
    return pl.pallas_call(
        functools.partial(score_kernel, n, cols, docs),
        name="scores",
        out_shape=jax.ShapeDtypeStruct((docs, store_rows.shape[0]), jnp.float32),
        in_specs=[anywhere] * 7,
        out_specs=pl.BlockSpec(memory_space=pltpu.VMEM),
        scratch_shapes=[
            pltpu.VMEM(activations.shape, jnp.bfloat16),
            pltpu.VMEM(gradients.shape, jnp.bfloat16),
            pltpu.VMEM(proj_in.shape[::-1], jnp.bfloat16),
            pltpu.VMEM(proj_out.shape[::-1], jnp.bfloat16),
            pltpu.VMEM(inverse.shape, jnp.float32),
            pltpu.VMEM(store_rows.shape, jnp.bfloat16),
            pltpu.VMEM(inverse.shape, jnp.bfloat16),
            pltpu.VMEM(inverse.shape, jnp.bfloat16),
            pltpu.VMEM(store_rows.shape[::-1], jnp.bfloat16),
            pltpu.VMEM((n, 1, tokens), jnp.int32),
            pltpu.VMEM((rank, tokens), jnp.float32),
            pltpu.VMEM((rank, tokens), jnp.float32),
            pltpu.VMEM((half, tokens), jnp.float32),
            pltpu.VMEM((rank, tokens), jnp.float32),
            pltpu.VMEM((half, tokens), jnp.float32),
            pltpu.VMEM((n * piece, LANES), jnp.float32),
            pltpu.VMEM((cols, doc_rows, width), jnp.float32),
            pltpu.VMEM((doc_rows, width), jnp.float32),
            pltpu.VMEM((n * cols, doc_rows, width), jnp.bfloat16),
            dma((5 + 2 * CHUNKS,)),
            dma((n,)), dma((n,)),
            dma((3,)), dma((3,)),
            dma((n,)), dma((n,)),
            dma((n * cols,)), dma((n * cols,)),
        ],
        compiler_params=pltpu.CompilerParams(
            collective_id=0, has_side_effects=True, vmem_limit_bytes=60 << 20
        ),
    )(activations, gradients, doc_ids[None, :], proj_in.T, proj_out.T, inverse, store_rows)


def suits_kernel(n, cols, activations, gradients, proj_in, inverse):
    rank = proj_in.shape[1]
    return (
        cols == 2
        and activations.shape[0] == LANES
        and LANES % rank == 0
        and (rank // cols * rank) % (8 * LANES) == 0
        and gradients.shape[1] % (CHUNKS * LANES) == 0
        and inverse.shape[1] % (cols * LANES) == 0
        and n <= 16
        and n & (n - 1) == 0
    )


def solution(mesh):
    in_specs = (
        P(("groups", "ctx"), "col"),
        P(("groups", "ctx"), "col"),
        P(("groups", "ctx")),
        P("col", None),
        P("col", None),
        P("col", "ctx"),
        P(("groups", "ctx", "col"), None),
    )
    out_specs = P(None, ("groups", "ctx", "col"))
    n, cols = mesh.shape["ctx"], mesh.shape["col"]

    def body(activations, gradients, doc_ids, proj_in, proj_out, inverse, store_rows):
        args = (activations, gradients, doc_ids, proj_in, proj_out, inverse, store_rows)
        if suits_kernel(n, cols, activations, gradients, proj_in, inverse):
            return fused(n, cols, *args)
        return shards(*args)

    return jax.shard_map(body, mesh=mesh, in_specs=in_specs, out_specs=out_specs, check_vma=False)
```

```python
import functools

import jax
import jax.numpy as jnp
from jax import lax
from jax.experimental import pallas as pl
from jax.experimental.pallas import tpu as pltpu
from jax.sharding import PartitionSpec as P


def from_behind(block, axis, distance):
    devices = range(lax.axis_size(axis))
    route = [(i - distance, i) for i in devices if i - distance in devices]
    return lax.ppermute(block, axis, route)


def shards(activations, gradients, doc_ids, proj_in, proj_out, inverse, store_rows):
    left_part = jnp.dot(activations, proj_in, preferred_element_type=jnp.float32)
    right_part = jnp.dot(gradients, proj_out, preferred_element_type=jnp.float32)
    proj_left, proj_right = lax.psum((left_part, right_part), "col")
    proj_rank = proj_right.shape[1]
    half_rank = proj_rank // lax.axis_size("col")
    own_half = lax.dynamic_slice_in_dim(proj_left, lax.axis_index("col") * half_rank, half_rank, 1)
    first_doc = doc_ids[0]
    slot_index = doc_ids - first_doc
    onehot = (slot_index[:, None] == jnp.arange(3, dtype=jnp.int32)[None, :]).astype(jnp.float32)
    weighted = (onehot[:, :, None] * own_half[:, None, :]).reshape(own_half.shape[0], 3 * half_rank)
    local_sums = lax.dot_general(
        weighted,
        proj_right,
        (((0,), (0,)), ((), ())),
        precision=lax.Precision.HIGHEST,
        preferred_element_type=jnp.float32,
    ).reshape(3, half_rank * proj_rank)
    doc_count = 3 * lax.axis_size("ctx") // 2
    last_row = lax.dynamic_index_in_dim(local_sums, slot_index[-1], 0, keepdims=False)
    incoming, incoming_id = from_behind((last_row, doc_ids[-1].astype(jnp.float32)), "ctx", 1)
    matches = (incoming_id == first_doc.astype(jnp.float32)).astype(jnp.float32)
    head_row = local_sums[0] + matches * incoming
    owned_rows = jnp.stack([head_row, local_sums[1]])
    owned_ids = (first_doc + jnp.arange(2, dtype=jnp.int32)).astype(jnp.float32)
    gathered, gathered_ids = (
        lax.all_gather(owned_rows, "ctx", axis=0, tiled=True),
        lax.all_gather(owned_ids, "ctx", axis=0, tiled=True),
    )
    positions = jnp.arange(gathered.shape[0], dtype=jnp.int32)
    wanted = jnp.arange(doc_count, dtype=jnp.int32).astype(jnp.float32)
    found = gathered_ids[None, :] == wanted[:, None]
    chosen = jnp.max(jnp.where(found, positions[None, :], -1), axis=1)
    doc_grads = jnp.take(gathered, chosen, axis=0)
    partial_q = jnp.dot(
        doc_grads, inverse, precision=lax.Precision.HIGHEST, preferred_element_type=jnp.float32
    )
    precond = lax.psum(partial_q, "col").astype(jnp.bfloat16)
    return lax.dot_general(
        lax.all_gather(precond, "ctx", axis=1, tiled=True),
        store_rows,
        (((1,), (1,)), ((), ())),
        preferred_element_type=jnp.float32,
    )


LANES = 128
SLOTS = 3
CHUNKS = 4
MESH = pl.DeviceIdType.MESH
def sums_order(n):
    order = []
    for r in range(1, n // 2 + 1):
        order += [n - r, r] if n - r != r else [r]
    return order


NT = (((1,), (1,)), ((), ()))


def halves(value):
    high = value.astype(jnp.bfloat16).astype(jnp.float32)
    return high, value - high


def dot_nt(left, right):
    return lax.dot_general(left, right, NT, preferred_element_type=jnp.float32)


def score_kernel(
    n, cols, docs,
    act, grad, ids, pin, pout, inv, store, out,
    act_v, grad_v, pin_v, pout_v, inv_v, store_v, inv_hi, inv_lo,
    store_t, ids_all, part_l, part_r, from_l, from_r, full_l, sums, q_part, q_from, q_all,
    load_sem, ids_send, ids_recv, pair_send, pair_recv, sums_send, sums_recv, q_send, q_recv,
):
    me = lax.axis_index("ctx")
    core = lax.axis_index("col")
    other = cols - 1 - core
    rank = pin.shape[0]
    half = rank // cols
    pack = LANES // rank
    groups = half // pack
    piece = SLOTS * groups
    width = q_part.shape[2]

    loads = [
        pltpu.make_async_copy(ids, ids_all.at[me], load_sem.at[0]),
        pltpu.make_async_copy(act, act_v, load_sem.at[1]),
        pltpu.make_async_copy(pin, pin_v, load_sem.at[2]),
    ]
    step = grad.shape[1] // CHUNKS
    for i in range(CHUNKS):
        span = pl.ds(i * step, step)
        loads.append(pltpu.make_async_copy(pout.at[:, span], pout_v.at[:, span], load_sem.at[3 + 2 * i]))
        loads.append(pltpu.make_async_copy(grad.at[:, span], grad_v.at[:, span], load_sem.at[4 + 2 * i]))
    loads.append(pltpu.make_async_copy(inv, inv_v, load_sem.at[3 + 2 * CHUNKS]))
    loads.append(pltpu.make_async_copy(store, store_v, load_sem.at[4 + 2 * CHUNKS]))
    for load in loads:
        load.start()

    barrier = pltpu.get_barrier_semaphore()
    ctx_peers = {r: {"ctx": jnp.bitwise_xor(me, r)} for r in sums_order(n)}
    peers = {}
    for r in range(n):
        for d in range(cols):
            if r or d:
                peers[cols * r + d] = {"ctx": lax.rem(me + r, n), "col": jnp.bitwise_xor(core, d)}
    for peer in peers.values():
        pl.semaphore_signal(barrier, inc=1, device_id=peer, device_id_type=MESH)

    loads[1].wait()
    loads[2].wait()
    part_l[...] = dot_nt(pin_v[...], act_v[...])

    def remote(src, dst, send, recv, peer):
        copy = pltpu.make_async_remote_copy(
            src_ref=src, dst_ref=dst, send_sem=send, recv_sem=recv, device_id=peer, device_id_type=MESH
        )
        copy.start()
        return copy

    right = None
    for i in range(CHUNKS):
        span = pl.ds(i * step, step)
        loads[3 + 2 * i].wait()
        loads[4 + 2 * i].wait()
        term = dot_nt(pout_v[:, span], grad_v[:, span])
        right = term if right is None else right + term
    part_r[...] = right
    pl.semaphore_wait(barrier, len(peers))
    partner = {"col": other}
    copy_l = remote(part_l.at[pl.ds(other * half, half)], from_l, pair_send.at[0], pair_recv.at[0], partner)
    copy_r = remote(part_r, from_r, pair_send.at[1], pair_recv.at[1], partner)
    ids_copies = [
        remote(ids, ids_all.at[me], ids_send.at[r], ids_recv.at[r], ctx_peers[r])
        for r in ctx_peers
    ]

    loads[0].wait()
    own_ids = ids_all[me]
    first = own_ids[:, 0:1]
    masks = [(own_ids == first + s).astype(jnp.float32) for s in range(SLOTS)]
    copy_l.wait_recv()
    full_l[...] = part_l[pl.ds(pl.multiple_of(core * half, half), half), :] + from_l[...]
    highs, lows = [], []
    for p in range(pack):
        rows = full_l[pl.ds(p, groups, stride=pack), :]
        high, low = halves(jnp.concatenate([rows * mask for mask in masks], axis=0))
        highs.append(high)
        lows.append(low)
    weights = jnp.concatenate(highs + highs + lows, axis=1).astype(jnp.bfloat16)
    copy_r.wait_recv()
    high, low = halves(part_r[...] + from_r[...])
    zero = jnp.zeros_like(high)

    def diagonal(block, p):
        return [block if q == p else zero for q in range(pack)]

    spread = jnp.concatenate(
        [
            jnp.concatenate(diagonal(high, p) + diagonal(low, p) + diagonal(high, p), axis=1)
            for p in range(pack)
        ],
        axis=0,
    ).astype(jnp.bfloat16)
    mine = pl.ds(pl.multiple_of(me * piece, 8), piece)
    sums[mine, :] = dot_nt(weights, spread)
    sums_copies = [
        remote(sums.at[mine], sums.at[mine], sums_send.at[r], sums_recv.at[r], ctx_peers[r])
        for r in ctx_peers
    ]

    loads[3 + 2 * CHUNKS].wait()
    band = LANES

    def split(i, carry):
        rows = pl.ds(pl.multiple_of(i * band, band), band)
        high, low = halves(inv_v[rows, :])
        inv_hi[rows, :] = high.astype(jnp.bfloat16)
        inv_lo[rows, :] = low.astype(jnp.bfloat16)
        return carry

    lax.fori_loop(0, inv_v.shape[0] // band, split, 0)
    loads[4 + 2 * CHUNKS].wait()
    store_t[...] = store_v[...].T

    for copy in ids_copies:
        copy.wait_recv()
    doc_rows = q_part.shape[1]
    column = lax.broadcasted_iota(jnp.int32, (1, SLOTS * n), 1)
    doc_of = jnp.zeros((1, SLOTS * n), jnp.int32)
    for b in range(n):
        inside = (column >= b * SLOTS) & (column < (b + 1) * SLOTS)
        doc_of = jnp.where(inside, ids_all[b][:, 0:1] + (column - b * SLOTS), doc_of)
    pick = (lax.broadcasted_iota(jnp.int32, (doc_rows, SLOTS * n), 0) == doc_of).astype(jnp.float32)

    for copy in sums_copies:
        copy.wait_recv()
    gathered = jnp.concatenate(
        [sums[pl.ds(k, SLOTS * n, stride=groups), :] for k in range(groups)], axis=1
    )
    high, low = halves(gathered)
    both = jnp.concatenate([high, low], axis=0).astype(jnp.bfloat16)
    main = jnp.dot(both, inv_hi[...], preferred_element_type=jnp.float32)
    rest = jnp.dot(high.astype(jnp.bfloat16), inv_lo[...], preferred_element_type=jnp.float32)
    rows = main[: SLOTS * n] + main[SLOTS * n :] + rest
    picked = jnp.dot(pick, rows, precision=lax.Precision.HIGHEST, preferred_element_type=jnp.float32)
    for c in range(cols):
        q_part[c] = picked[:, c * width : (c + 1) * width]
    copy_q = remote(q_part.at[other], q_from, pair_send.at[2], pair_recv.at[2], partner)
    copy_q.wait_recv()
    slot = me * cols + core
    q_all[slot] = (q_part[core] + q_from[...]).astype(jnp.bfloat16)
    q_copies = [
        remote(q_all.at[slot], q_all.at[slot], q_send.at[i], q_recv.at[i], peers[i])
        for i in peers
    ]
    for copy in q_copies:
        copy.wait_recv()
    precond = jnp.concatenate([q_all[i] for i in range(n * cols)], axis=1)
    out[...] = jnp.dot(precond, store_t[...], preferred_element_type=jnp.float32)[:docs]
    for copy in [copy_l, copy_r, copy_q] + ids_copies + sums_copies + q_copies:
        copy.wait_send()


def fused(n, cols, activations, gradients, doc_ids, proj_in, proj_out, inverse, store_rows):
    tokens = activations.shape[0]
    rank = proj_in.shape[1]
    half = rank // cols
    docs = SLOTS * n // 2
    doc_rows = -(-docs // 16) * 16
    width = inverse.shape[1] // cols
    piece = SLOTS * half * rank // LANES
    anywhere = pl.BlockSpec(memory_space=pl.ANY)
    dma = pltpu.SemaphoreType.DMA
    return pl.pallas_call(
        functools.partial(score_kernel, n, cols, docs),
        name="scores",
        out_shape=jax.ShapeDtypeStruct((docs, store_rows.shape[0]), jnp.float32),
        in_specs=[anywhere] * 7,
        out_specs=pl.BlockSpec(memory_space=pltpu.VMEM),
        scratch_shapes=[
            pltpu.VMEM(activations.shape, jnp.bfloat16),
            pltpu.VMEM(gradients.shape, jnp.bfloat16),
            pltpu.VMEM(proj_in.shape[::-1], jnp.bfloat16),
            pltpu.VMEM(proj_out.shape[::-1], jnp.bfloat16),
            pltpu.VMEM(inverse.shape, jnp.float32),
            pltpu.VMEM(store_rows.shape, jnp.bfloat16),
            pltpu.VMEM(inverse.shape, jnp.bfloat16),
            pltpu.VMEM(inverse.shape, jnp.bfloat16),
            pltpu.VMEM(store_rows.shape[::-1], jnp.bfloat16),
            pltpu.VMEM((n, 1, tokens), jnp.int32),
            pltpu.VMEM((rank, tokens), jnp.float32),
            pltpu.VMEM((rank, tokens), jnp.float32),
            pltpu.VMEM((half, tokens), jnp.float32),
            pltpu.VMEM((rank, tokens), jnp.float32),
            pltpu.VMEM((half, tokens), jnp.float32),
            pltpu.VMEM((n * piece, LANES), jnp.float32),
            pltpu.VMEM((cols, doc_rows, width), jnp.float32),
            pltpu.VMEM((doc_rows, width), jnp.float32),
            pltpu.VMEM((n * cols, doc_rows, width), jnp.bfloat16),
            dma((5 + 2 * CHUNKS,)),
            dma((n,)), dma((n,)),
            dma((3,)), dma((3,)),
            dma((n,)), dma((n,)),
            dma((n * cols,)), dma((n * cols,)),
        ],
        compiler_params=pltpu.CompilerParams(
            collective_id=0, has_side_effects=True, vmem_limit_bytes=60 << 20
        ),
    )(activations, gradients, doc_ids[None, :], proj_in.T, proj_out.T, inverse, store_rows)


def suits_kernel(n, cols, activations, gradients, proj_in, inverse):
    rank = proj_in.shape[1]
    return (
        cols == 2
        and activations.shape[0] == LANES
        and LANES % rank == 0
        and (rank // cols * rank) % (8 * LANES) == 0
        and gradients.shape[1] % (CHUNKS * LANES) == 0
        and inverse.shape[1] % (cols * LANES) == 0
        and n <= 16
        and n & (n - 1) == 0
    )


def solution(mesh):
    in_specs = (
        P(("groups", "ctx"), "col"),
        P(("groups", "ctx"), "col"),
        P(("groups", "ctx")),
        P("col", None),
        P("col", None),
        P("col", "ctx"),
        P(("groups", "ctx", "col"), None),
    )
    out_specs = P(None, ("groups", "ctx", "col"))
    n, cols = mesh.shape["ctx"], mesh.shape["col"]

    def body(activations, gradients, doc_ids, proj_in, proj_out, inverse, store_rows):
        args = (activations, gradients, doc_ids, proj_in, proj_out, inverse, store_rows)
        if suits_kernel(n, cols, activations, gradients, proj_in, inverse):
            return fused(n, cols, *args)
        return shards(*args)

    return jax.shard_map(body, mesh=mesh, in_specs=in_specs, out_specs=out_specs, check_vma=False)
```
